32 devices in a mesh: shard: 4 (over z), tensor: 2 (over y), section: 4 (over x, core).
Axes of the slice: x: 2, y: 2, z: 4, core: 2. Of those that a mesh axis runs over, the one named last changes fastest.
Arguments:
- qkv_grad: bfloat16 [4, 4096, 6144], P('shard', 'section', 'tensor'), may hold values from -150 to 150
- master: float32 [4096, 6144], P(('section', 'shard', 'tensor')), may hold values from -3 to 3
- moment_one: float32 [4096, 6144], P(('section', 'shard', 'tensor')), may hold values from -3 to 3
- moment_two: float32 [4096, 6144], P(('section', 'shard', 'tensor')), may hold values from 0.05 to 2
- average: float32 [4096, 6144], P(('section', 'shard'), 'tensor'), may hold values from -3 to 3
- step: int32 [], replicated, may hold values from 1 to 20
Outputs:
- weights: bfloat16 [4096, 6144], P('section', 'tensor')
- new_master: float32 [4096, 6144], P(('section', 'shard', 'tensor'))
- new_one: float32 [4096, 6144], P(('section', 'shard', 'tensor'))
- new_two: float32 [4096, 6144], P(('section', 'shard', 'tensor'))
- new_average: float32 [4096, 6144], P(('section', 'shard'), 'tensor')
The draws below stay inside these ranges and needn't reach their ends.
All inputs are finite; a program needn't handle non-finite values.
Results may differ from the reference program's by a relative error of at most 0.0035.
Values may be sent and summed in bfloat16 or wider, within the bound.
A program may use at most 128 MiB of HBM per device.

```python
import math
import jax
import jax.numpy as jnp
from jax import lax

D = 4096
QKV = 6144
REPLICAS = 4


def draw_qkv_grad(key, part):
    base = jax.random.fold_in(key, 11)
    first, second, third = jax.random.split(base, 3)
    rows = jnp.arange(D).astype(jnp.float32)
    row_scale = jnp.power(jnp.float32(3.0), rows / D) * jnp.exp(jax.random.uniform(first, (D,), jnp.float32) * math.log(10.0))
    col_scale = jnp.exp(jax.random.uniform(second, (QKV,), jnp.float32) * math.log(10.0))
    noise = jnp.clip(jax.random.normal(third, (REPLICAS, D, QKV), jnp.float32), -5.0, 5.0)
    values = jnp.clip(noise * row_scale[None, :, None] * col_scale[None, None, :], -150.0, 150.0)
    return values.astype(jnp.bfloat16)


def levels(rng, extent, cuts, least, high):
    def one(dim, shards_of):
        draws = jax.random.uniform(jax.random.fold_in(jax.random.fold_in(rng, 6), dim), (shards_of,), jnp.float32, least / len(cuts), high / len(cuts))
        return jnp.repeat(jnp.exp(draws), extent[dim] // shards_of).reshape((-1,) + (1,) * (len(extent) - dim - 1))

    level = one(*cuts[0])
    for cut in cuts[1:]:
        level = level * one(*cut)
    return level


def centred(key, dims, width, reach, cuts=(), kind=jnp.bfloat16):
    entries = width * jax.random.normal(key, dims, jnp.float32)
    if cuts:
        entries = entries * levels(key, dims, cuts, -0.22, 0.18)
    return jnp.clip(entries, -reach, reach).astype(kind)


def setup_inputs(seed: int = 0) -> dict:
    key_list = jax.random.split(jax.random.key(seed), 7)
    return {
        "qkv_grad": draw_qkv_grad(jax.random.fold_in(key_list[6], 71), 0),
        "master": centred(key_list[1], (D, QKV), 0.5, 3.0, ((0, 32),), jnp.float32),
        "moment_one": centred(key_list[2], (D, QKV), 0.5, 3.0, ((0, 32),), jnp.float32),
        "moment_two": jnp.clip(jnp.exp(math.log(2.0) - 3.6888794 * jax.random.uniform(key_list[3], (D, QKV), jnp.float32) ** levels(key_list[3], (D, QKV), ((0, 32),), -0.2, 0.2)), 0.05, 2.0),
        "average": centred(key_list[4], (D, QKV), 0.5, 3.0, ((0, 16), (1, 2)), jnp.float32),
        "step": jax.random.randint(key_list[5], (), 1, 21).astype(jnp.int32),
    }


def reference(qkv_grad, master, moment_one, moment_two, average, step):
    grad = lax.optimization_barrier(jnp.sum(qkv_grad.astype(jnp.float32), axis=0))
    sumsq = jnp.sum(grad * grad)
    limit = jnp.float32(math.sqrt(D * QKV))
    clip = jnp.minimum(jnp.float32(1.0), limit / (jnp.sqrt(sumsq) + 1e-06))
    clipped = clip * grad
    new_one = 0.9 * moment_one + 0.1 * clipped
    new_two = 0.95 * moment_two + 0.05 * clipped * clipped
    count = step.astype(jnp.float32)
    first_fix = 1.0 - jnp.power(jnp.float32(0.9), count)
    second_fix = 1.0 - jnp.power(jnp.float32(0.95), count)
    update = new_one / first_fix / (jnp.sqrt(new_two / second_fix) + 1e-08)
    new_master = master * (1.0 - 0.1 * 0.1) - 0.1 * update
    weights = new_master.astype(jnp.bfloat16)
    new_average = 0.99 * average + 0.01 * new_master
    return (weights, new_master, new_one, new_two, new_average)
```

```python
import functools
import math

import jax
import jax.numpy as jnp
from jax import lax
from jax.experimental import pallas as pl
from jax.experimental.pallas import tpu as pltpu
from jax.sharding import PartitionSpec as P

D = 4096
QKV = 6144


def update_kernel(pos, scal, grad, master, one, two, out_master, out_one, out_two, out_half):
    clip, first_fix, second_fix = scal[0], scal[1], scal[2]
    clipped = clip * grad[0].astype(jnp.float32)
    new_one = 0.9 * one[...] + 0.1 * clipped
    new_two = 0.95 * two[...] + 0.05 * clipped * clipped
    update = new_one / first_fix / (jnp.sqrt(new_two / second_fix) + 1e-08)
    new_master = master[...] * (1.0 - 0.1 * 0.1) - 0.1 * update
    out_one[...] = new_one
    out_two[...] = new_two
    out_master[...] = new_master
    out_half[0] = new_master.astype(jnp.bfloat16)


def update(pos, scal, grads, master, one, two):
    groups, rows, cols = grads.shape
    tile = min(rows, 32)
    state = pl.BlockSpec((tile, cols), lambda k, r, p: (r, lax.rem(p[0] - k + groups, groups)))
    piece = pl.BlockSpec((1, tile, cols), lambda k, r, p: (k, r, 0))
    return pl.pallas_call(
        update_kernel,
        grid_spec=pltpu.PrefetchScalarGridSpec(
            num_scalar_prefetch=1,
            grid=(groups, rows // tile),
            in_specs=[pl.BlockSpec(memory_space=pltpu.SMEM), piece, state, state, state],
            out_specs=[state, state, state, piece],
        ),
        out_shape=[jax.ShapeDtypeStruct(master.shape, jnp.float32)] * 3
        + [jax.ShapeDtypeStruct(grads.shape, jnp.bfloat16)],
        compiler_params=pltpu.CompilerParams(vmem_limit_bytes=32 * 2**20),
        cost_estimate=pl.CostEstimate(flops=master.size * 16, bytes_accessed=master.size * 28, transcendentals=0),
    )(pos, scal, grads, master, one, two)


def place_kernel(pos, piece, *refs):
    refs[-1][...] = piece[...].reshape(refs[-1].shape)


def place(pos, piece, groups, k, held):
    blocks, rows, cols = piece.shape
    in_specs = [pl.BlockSpec((1, rows, cols), lambda s, p: (s, 0, 0))]
    args = [piece]
    aliases = {}
    if held is not None:
        in_specs.append(pl.BlockSpec(memory_space=pl.ANY))
        args.append(held)
        aliases = {2: 0}
    return pl.pallas_call(
        place_kernel,
        grid_spec=pltpu.PrefetchScalarGridSpec(
            num_scalar_prefetch=1,
            grid=(blocks,),
            in_specs=in_specs,
            out_specs=pl.BlockSpec((1, 1, rows, cols), lambda s, p: (s, lax.rem(p[0] + k, groups), 0, 0)),
        ),
        out_shape=jax.ShapeDtypeStruct((blocks, groups, rows, cols), piece.dtype),
        input_output_aliases=aliases,
        cost_estimate=pl.CostEstimate(flops=0, bytes_accessed=piece.size * 4, transcendentals=0),
    )(pos, *args)


def average_kernel(pos, fresh, average, *refs):
    refs[-1][...] = 0.99 * average[...] + 0.01 * fresh[...].astype(jnp.float32)


def average_step(pos, fresh, average, groups, k, held):
    rows, cols = fresh.shape
    block = pl.BlockSpec((rows, cols), lambda i, p: (lax.rem(p[0] + k, groups), 0))
    in_specs = [pl.BlockSpec((rows, cols), lambda i, p: (0, 0)), block]
    args = [fresh, average]
    aliases = {}
    if held is not None:
        in_specs.append(pl.BlockSpec(memory_space=pl.ANY))
        args.append(held)
        aliases = {3: 0}
    return pl.pallas_call(
        average_kernel,
        grid_spec=pltpu.PrefetchScalarGridSpec(
            num_scalar_prefetch=1, grid=(1,), in_specs=in_specs, out_specs=block
        ),
        out_shape=jax.ShapeDtypeStruct(average.shape, jnp.float32),
        input_output_aliases=aliases,
        compiler_params=pltpu.CompilerParams(vmem_limit_bytes=32 * 2**20),
        cost_estimate=pl.CostEstimate(flops=fresh.size * 3, bytes_accessed=fresh.size * 10, transcendentals=0),
    )(pos, *args)


def body(shards, groups, qkv_grad, master, moment_one, moment_two, average, step):
    t = lax.axis_index("tensor")
    pos = jnp.reshape(t, (1,)).astype(jnp.int32)
    rows = qkv_grad.shape[1] // (shards * groups)
    cols = qkv_grad.shape[2]
    blocks = qkv_grad.reshape(shards, groups, rows, cols)
    pieces = [None] * groups
    local_sq = jnp.float32(0.0)
    for k in range(groups - 1, -1, -1):
        block = lax.dynamic_index_in_dim(blocks, lax.rem(t + k, groups), 1, keepdims=False)
        share = lax.psum_scatter(
            block.reshape(shards * rows, cols), "shard", scatter_dimension=0, tiled=True
        )
        wide = share.astype(jnp.float32)
        local_sq = local_sq + jnp.sum(wide * wide)
        if k:
            share = lax.ppermute(share, "tensor", [(i, (i + k) % groups) for i in range(groups)])
        pieces[k] = share
    sumsq = lax.psum(local_sq, ("shard", "tensor", "section"))
    limit = jnp.float32(math.sqrt(D * QKV))
    clip = jnp.minimum(jnp.float32(1.0), limit / (jnp.sqrt(sumsq) + 1e-06))
    count = step.astype(jnp.float32)
    first_fix = 1.0 - jnp.power(jnp.float32(0.9), count)
    second_fix = 1.0 - jnp.power(jnp.float32(0.95), count)
    scal = jnp.stack([clip, first_fix, second_fix])
    new_master, new_one, new_two, half = update(
        pos, scal, jnp.stack(pieces), master, moment_one, moment_two
    )
    weights = None
    new_average = None
    for k in range(groups):
        piece = half[k]
        if k:
            piece = lax.ppermute(piece, "tensor", [(i, (i - k) % groups) for i in range(groups)])
        gathered = lax.all_gather(piece, "shard", axis=0, tiled=False)
        new_average = average_step(pos, piece, average, groups, k, new_average)
        weights = place(pos, gathered, groups, k, weights)
    return (weights.reshape(shards * groups * rows, cols), new_master, new_one, new_two, new_average)


def solution(mesh):
    state = P(("section", "shard", "tensor"), None)
    in_specs = (
        P("shard", "section", "tensor"),
        state,
        state,
        state,
        P(("section", "shard"), "tensor"),
        P(),
    )
    out_specs = (
        P("section", "tensor"),
        state,
        state,
        state,
        P(("section", "shard"), "tensor"),
    )
    fn = functools.partial(body, mesh.shape["shard"], mesh.shape["tensor"])
    return jax.shard_map(fn, mesh=mesh, in_specs=in_specs, out_specs=out_specs, check_vma=False)
```

```python
import functools
import math

import jax
import jax.numpy as jnp
from jax import lax
from jax.experimental import pallas as pl
from jax.experimental.pallas import tpu as pltpu
from jax.sharding import PartitionSpec as P

D = 4096
QKV = 6144


def update_kernel(pos, scal, grad, master, one, two, out_master, out_one, out_two, out_half):
    clip, first_fix, second_fix = scal[0], scal[1], scal[2]
    clipped = clip * grad[0].astype(jnp.float32)
    new_one = 0.9 * one[...] + 0.1 * clipped
    new_two = 0.95 * two[...] + 0.05 * clipped * clipped
    update = new_one / first_fix / (jnp.sqrt(new_two / second_fix) + 1e-08)
    new_master = master[...] * (1.0 - 0.1 * 0.1) - 0.1 * update
    out_one[...] = new_one
    out_two[...] = new_two
    out_master[...] = new_master
    out_half[0] = new_master.astype(jnp.bfloat16)


def update(pos, scal, grads, master, one, two):
    groups, rows, cols = grads.shape
    tile = min(rows, 32)
    state = pl.BlockSpec((tile, cols), lambda k, r, p: (r, lax.rem(p[0] - k + groups, groups)))
    piece = pl.BlockSpec((1, tile, cols), lambda k, r, p: (k, r, 0))
    return pl.pallas_call(
        update_kernel,
        grid_spec=pltpu.PrefetchScalarGridSpec(
            num_scalar_prefetch=1,
            grid=(groups, rows // tile),
            in_specs=[pl.BlockSpec(memory_space=pltpu.SMEM), piece, state, state, state],
            out_specs=[state, state, state, piece],
        ),
        out_shape=[jax.ShapeDtypeStruct(master.shape, jnp.float32)] * 3
        + [jax.ShapeDtypeStruct(grads.shape, jnp.bfloat16)],
        compiler_params=pltpu.CompilerParams(vmem_limit_bytes=32 * 2**20),
        cost_estimate=pl.CostEstimate(flops=master.size * 16, bytes_accessed=master.size * 28, transcendentals=0),
    )(pos, scal, grads, master, one, two)


def place_kernel(pos, piece, *refs):
    refs[-1][...] = piece[...].reshape(refs[-1].shape)


def place(pos, piece, groups, k, held):
    blocks, rows, cols = piece.shape
    in_specs = [pl.BlockSpec((1, rows, cols), lambda s, p: (s, 0, 0))]
    args = [piece]
    aliases = {}
    if held is not None:
        in_specs.append(pl.BlockSpec(memory_space=pl.ANY))
        args.append(held)
        aliases = {2: 0}
    return pl.pallas_call(
        place_kernel,
        grid_spec=pltpu.PrefetchScalarGridSpec(
            num_scalar_prefetch=1,
            grid=(blocks,),
            in_specs=in_specs,
            out_specs=pl.BlockSpec((1, 1, rows, cols), lambda s, p: (s, lax.rem(p[0] + k, groups), 0, 0)),
        ),
        out_shape=jax.ShapeDtypeStruct((blocks, groups, rows, cols), piece.dtype),
        input_output_aliases=aliases,
        cost_estimate=pl.CostEstimate(flops=0, bytes_accessed=piece.size * 4, transcendentals=0),
    )(pos, *args)


def average_kernel(pos, fresh, average, *refs):
    refs[-1][...] = 0.99 * average[...] + 0.01 * fresh[...].astype(jnp.float32)


def average_step(pos, fresh, average, groups, k, held):
    rows, cols = fresh.shape
    block = pl.BlockSpec((rows, cols), lambda i, p: (lax.rem(p[0] + k, groups), 0))
    in_specs = [pl.BlockSpec((rows, cols), lambda i, p: (0, 0)), block]
    args = [fresh, average]
    aliases = {}
    if held is not None:
        in_specs.append(pl.BlockSpec(memory_space=pl.ANY))
        args.append(held)
        aliases = {3: 0}
    return pl.pallas_call(
        average_kernel,
        grid_spec=pltpu.PrefetchScalarGridSpec(
            num_scalar_prefetch=1, grid=(1,), in_specs=in_specs, out_specs=block
        ),
        out_shape=jax.ShapeDtypeStruct(average.shape, jnp.float32),
        input_output_aliases=aliases,
        compiler_params=pltpu.CompilerParams(vmem_limit_bytes=32 * 2**20),
        cost_estimate=pl.CostEstimate(flops=fresh.size * 3, bytes_accessed=fresh.size * 10, transcendentals=0),
    )(pos, *args)


MESH = pl.DeviceIdType.MESH


def total_kernel(axes, x_ref, out_ref, held, send_sem, recv_sem):
    barrier = pltpu.get_barrier_semaphore()
    count = 0
    for name, size in axes:
        me = lax.axis_index(name)
        for off in range(1, size):
            pl.semaphore_signal(
                barrier, inc=1, device_id={name: lax.rem(me + off, size)}, device_id_type=MESH
            )
            count += 1
    pl.semaphore_wait(barrier, count)
    at = 0
    own = x_ref[...]
    for name, size in axes:
        me = lax.axis_index(name)
        held[at] = own
        copies = []
        for off in range(1, size):
            copy = pltpu.make_async_remote_copy(
                src_ref=held.at[at],
                dst_ref=held.at[at + off],
                send_sem=send_sem.at[at + off],
                recv_sem=recv_sem.at[at + off],
                device_id={name: lax.rem(me + off, size)},
                device_id_type=MESH,
            )
            copy.start()
            copies.append(copy)
        for off, copy in enumerate(copies, 1):
            copy.wait()
            own = own + held[at + off]
        at += size
    out_ref[...] = own


def total(axes, value):
    slots = sum(size for _, size in axes)
    return pl.pallas_call(
        functools.partial(total_kernel, axes),
        out_shape=jax.ShapeDtypeStruct((8, 128), jnp.float32),
        in_specs=[pl.BlockSpec(memory_space=pltpu.VMEM)],
        out_specs=pl.BlockSpec(memory_space=pltpu.VMEM),
        scratch_shapes=[
            pltpu.VMEM((slots, 8, 128), jnp.float32),
            pltpu.SemaphoreType.DMA((slots,)),
            pltpu.SemaphoreType.DMA((slots,)),
        ],
        compiler_params=pltpu.CompilerParams(collective_id=0, has_side_effects=True),
    )(jnp.full((8, 128), value, jnp.float32))[0, 0]


def body(axes, qkv_grad, master, moment_one, moment_two, average, step):
    shards, groups = dict(axes)["shard"], dict(axes)["tensor"]
    t = lax.axis_index("tensor")
    pos = jnp.reshape(t, (1,)).astype(jnp.int32)
    rows = qkv_grad.shape[1] // (shards * groups)
    cols = qkv_grad.shape[2]
    blocks = qkv_grad.reshape(shards, groups, rows, cols)
    pieces = [None] * groups
    local_sq = jnp.float32(0.0)
    for k in range(groups - 1, -1, -1):
        block = lax.dynamic_index_in_dim(blocks, lax.rem(t + k, groups), 1, keepdims=False)
        share = lax.psum_scatter(
            block.reshape(shards * rows, cols), "shard", scatter_dimension=0, tiled=True
        )
        wide = share.astype(jnp.float32)
        local_sq = local_sq + jnp.sum(wide * wide)
        if k:
            share = lax.ppermute(share, "tensor", [(i, (i + k) % groups) for i in range(groups)])
        pieces[k] = share
    sumsq = total(axes, local_sq)
    limit = jnp.float32(math.sqrt(D * QKV))
    clip = jnp.minimum(jnp.float32(1.0), limit / (jnp.sqrt(sumsq) + 1e-06))
    count = step.astype(jnp.float32)
    first_fix = 1.0 - jnp.power(jnp.float32(0.9), count)
    second_fix = 1.0 - jnp.power(jnp.float32(0.95), count)
    scal = jnp.stack([clip, first_fix, second_fix])
    new_master, new_one, new_two, half = update(
        pos, scal, jnp.stack(pieces), master, moment_one, moment_two
    )
    weights = None
    new_average = None
    for k in range(groups):
        piece = half[k]
        if k:
            piece = lax.ppermute(piece, "tensor", [(i, (i - k) % groups) for i in range(groups)])
        gathered = lax.all_gather(piece, "shard", axis=0, tiled=False)
        new_average = average_step(pos, piece, average, groups, k, new_average)
        weights = place(pos, gathered, groups, k, weights)
    return (weights.reshape(shards * groups * rows, cols), new_master, new_one, new_two, new_average)


def solution(mesh):
    state = P(("section", "shard", "tensor"), None)
    in_specs = (
        P("shard", "section", "tensor"),
        state,
        state,
        state,
        P(("section", "shard"), "tensor"),
        P(),
    )
    out_specs = (
        P("section", "tensor"),
        state,
        state,
        state,
        P(("section", "shard"), "tensor"),
    )
    fn = functools.partial(body, [(name, mesh.shape[name]) for name in ("tensor", "section", "shard")])
    return jax.shard_map(fn, mesh=mesh, in_specs=in_specs, out_specs=out_specs, check_vma=False)
```

```python
import functools
import math

import jax
import jax.numpy as jnp
from jax import lax
from jax.experimental import pallas as pl
from jax.experimental.pallas import tpu as pltpu
from jax.sharding import PartitionSpec as P

D = 4096
QKV = 6144


def update_kernel(pos, scal, grad, master, one, two, out_master, out_one, out_two, out_half):
    clip, first_fix, second_fix = scal[0], scal[1], scal[2]
    clipped = clip * grad[0].astype(jnp.float32)
    new_one = 0.9 * one[...] + 0.1 * clipped
    new_two = 0.95 * two[...] + 0.05 * clipped * clipped
    update = new_one / first_fix / (jnp.sqrt(new_two / second_fix) + 1e-08)
    new_master = master[...] * (1.0 - 0.1 * 0.1) - 0.1 * update
    out_one[...] = new_one
    out_two[...] = new_two
    out_master[...] = new_master
    out_half[0] = new_master.astype(jnp.bfloat16)


def update(pos, scal, grads, master, one, two):
    groups, rows, cols = grads.shape
    tile = min(rows, 32)
    state = pl.BlockSpec((tile, cols), lambda k, r, p: (r, lax.rem(p[0] - k + groups, groups)))
    piece = pl.BlockSpec((1, tile, cols), lambda k, r, p: (k, r, 0))
    return pl.pallas_call(
        update_kernel,
        grid_spec=pltpu.PrefetchScalarGridSpec(
            num_scalar_prefetch=1,
            grid=(groups, rows // tile),
            in_specs=[pl.BlockSpec(memory_space=pltpu.SMEM), piece, state, state, state],
            out_specs=[state, state, state, piece],
        ),
        out_shape=[jax.ShapeDtypeStruct(master.shape, jnp.float32)] * 3
        + [jax.ShapeDtypeStruct(grads.shape, jnp.bfloat16)],
        compiler_params=pltpu.CompilerParams(vmem_limit_bytes=32 * 2**20),
        cost_estimate=pl.CostEstimate(flops=master.size * 16, bytes_accessed=master.size * 28, transcendentals=0),
    )(pos, scal, grads, master, one, two)


MESH = pl.DeviceIdType.MESH


def total_kernel(axes, x_ref, out_ref, held, send_sem, recv_sem):
    barrier = pltpu.get_barrier_semaphore()
    count = 0
    for name, size in axes:
        me = lax.axis_index(name)
        for off in range(1, size):
            pl.semaphore_signal(
                barrier, inc=1, device_id={name: lax.rem(me + off, size)}, device_id_type=MESH
            )
            count += 1
    pl.semaphore_wait(barrier, count)
    at = 0
    own = x_ref[...]
    for name, size in axes:
        me = lax.axis_index(name)
        held[at] = own
        copies = []
        for off in range(1, size):
            copy = pltpu.make_async_remote_copy(
                src_ref=held.at[at],
                dst_ref=held.at[at + off],
                send_sem=send_sem.at[at + off],
                recv_sem=recv_sem.at[at + off],
                device_id={name: lax.rem(me + off, size)},
                device_id_type=MESH,
            )
            copy.start()
            copies.append(copy)
        for off, copy in enumerate(copies, 1):
            copy.wait()
            own = own + held[at + off]
        at += size
    out_ref[...] = own


def total(axes, value):
    slots = sum(size for _, size in axes)
    return pl.pallas_call(
        functools.partial(total_kernel, axes),
        out_shape=jax.ShapeDtypeStruct((8, 128), jnp.float32),
        in_specs=[pl.BlockSpec(memory_space=pltpu.VMEM)],
        out_specs=pl.BlockSpec(memory_space=pltpu.VMEM),
        scratch_shapes=[
            pltpu.VMEM((slots, 8, 128), jnp.float32),
            pltpu.SemaphoreType.DMA((slots,)),
            pltpu.SemaphoreType.DMA((slots,)),
        ],
        compiler_params=pltpu.CompilerParams(collective_id=0, has_side_effects=True),
    )(jnp.full((8, 128), value, jnp.float32))[0, 0]


def spread_kernel(shards, groups, half, out, y_send, y_recv, z_send, z_recv, own_sem):
    s = lax.axis_index("shard")
    t = lax.axis_index("tensor")
    last = shards - 1
    barrier = pltpu.get_barrier_semaphore()
    for off in range(1, groups):
        pl.semaphore_signal(
            barrier, inc=1, device_id={"tensor": lax.rem(t + off, groups)}, device_id_type=MESH
        )

    @pl.when(s < last)
    def _():
        pl.semaphore_signal(barrier, inc=1, device_id={"shard": s + 1}, device_id_type=MESH)

    @pl.when(s > 0)
    def _():
        pl.semaphore_signal(barrier, inc=1, device_id={"shard": s - 1}, device_id_type=MESH)

    peers = groups - 1 + jnp.minimum(s, 1) + jnp.minimum(last - s, 1)
    pl.semaphore_wait(barrier, peers)

    def across(k):
        return pltpu.make_async_remote_copy(
            src_ref=half.at[k],
            dst_ref=out.at[s, t],
            send_sem=y_send.at[k],
            recv_sem=y_recv.at[k],
            device_id={"tensor": lax.rem(t - k + groups, groups)},
            device_id_type=MESH,
        )

    def hop(way, k, d):
        slot = s - d if way == 0 else s + d
        group = lax.rem(t + k, groups)
        return pltpu.make_async_remote_copy(
            src_ref=half.at[0] if k == 0 and d == 0 else out.at[slot, group],
            dst_ref=out.at[slot, group],
            send_sem=z_send.at[way, k, d],
            recv_sem=z_recv.at[way, k, d],
            device_id={"shard": s + 1 if way == 0 else s - 1},
            device_id_type=MESH,
        )

    def arrival(way, k, d):
        slot = s - d if way == 0 else s + d
        group = lax.rem(t + k, groups)
        return pltpu.make_async_remote_copy(
            src_ref=out.at[slot, group],
            dst_ref=out.at[slot, group],
            send_sem=z_send.at[way, k, d - 1],
            recv_sem=z_recv.at[way, k, d - 1],
            device_id={"shard": s - 1 if way == 0 else s + 1},
            device_id_type=MESH,
        )

    def sends(way, d):
        if way == 0:
            return jnp.logical_and(s >= d, s < last)
        return jnp.logical_and(s + d <= last, s > 0)

    def gets(way, d):
        return s >= d if way == 0 else s + d <= last

    order = sorted(((k, d) for k in range(groups) for d in range(shards)), key=lambda e: (e[0] + e[1], e[0]))
    for k, d in order:
        if d == 0 and k:
            landed = pltpu.make_async_remote_copy(
                src_ref=half.at[k],
                dst_ref=out.at[s, lax.rem(t + k, groups)],
                send_sem=y_send.at[k],
                recv_sem=y_recv.at[k],
                device_id={"tensor": lax.rem(t + k, groups)},
                device_id_type=MESH,
            )
            landed.wait_recv()
        for way in (0, 1):
            if d:
                @pl.when(gets(way, d))
                def _():
                    arrival(way, k, d).wait_recv()
            if d < last:
                @pl.when(sends(way, d))
                def _():
                    hop(way, k, d).start()
        if d == 0 and k == 0:
            for j in range(1, groups):
                across(j).start()
            pltpu.make_async_copy(half.at[0], out.at[s, t], own_sem).start()
    pltpu.make_async_copy(half.at[0], out.at[s, t], own_sem).wait()
    for k, d in order:
        if d == 0 and k:
            across(k).wait_send()
        for way in (0, 1):
            if d < last:
                @pl.when(sends(way, d))
                def _():
                    hop(way, k, d).wait_send()


def spread(shards, groups, half):
    _, rows, cols = half.shape
    return pl.pallas_call(
        functools.partial(spread_kernel, shards, groups),
        out_shape=jax.ShapeDtypeStruct((shards, groups, rows, cols), half.dtype),
        in_specs=[pl.BlockSpec(memory_space=pl.ANY)],
        out_specs=pl.BlockSpec(memory_space=pl.ANY),
        scratch_shapes=[
            pltpu.SemaphoreType.DMA((groups,)),
            pltpu.SemaphoreType.DMA((groups,)),
            pltpu.SemaphoreType.DMA((2, groups, shards)),
            pltpu.SemaphoreType.DMA((2, groups, shards)),
            pltpu.SemaphoreType.DMA,
        ],
        compiler_params=pltpu.CompilerParams(collective_id=1, has_side_effects=True),
    )(half)


def body(axes, qkv_grad, master, moment_one, moment_two, average, step):
    shards, groups = dict(axes)["shard"], dict(axes)["tensor"]
    t = lax.axis_index("tensor")
    pos = jnp.reshape(t, (1,)).astype(jnp.int32)
    rows = qkv_grad.shape[1] // (shards * groups)
    cols = qkv_grad.shape[2]
    blocks = qkv_grad.reshape(shards, groups, rows, cols)
    pieces = [None] * groups
    local_sq = jnp.float32(0.0)
    for k in range(groups - 1, -1, -1):
        block = lax.dynamic_index_in_dim(blocks, lax.rem(t + k, groups), 1, keepdims=False)
        share = lax.psum_scatter(
            block.reshape(shards * rows, cols), "shard", scatter_dimension=0, tiled=True
        )
        wide = share.astype(jnp.float32)
        local_sq = local_sq + jnp.sum(wide * wide)
        if k:
            share = lax.ppermute(share, "tensor", [(i, (i + k) % groups) for i in range(groups)])
        pieces[k] = share
    sumsq = total(axes, local_sq)
    limit = jnp.float32(math.sqrt(D * QKV))
    clip = jnp.minimum(jnp.float32(1.0), limit / (jnp.sqrt(sumsq) + 1e-06))
    count = step.astype(jnp.float32)
    first_fix = 1.0 - jnp.power(jnp.float32(0.9), count)
    second_fix = 1.0 - jnp.power(jnp.float32(0.95), count)
    scal = jnp.stack([clip, first_fix, second_fix])
    new_master, new_one, new_two, half = update(
        pos, scal, jnp.stack(pieces), master, moment_one, moment_two
    )
    weights = spread(shards, groups, half)
    fresh = lax.dynamic_index_in_dim(weights, lax.axis_index("shard"), 0, keepdims=False)
    new_average = 0.99 * average + 0.01 * fresh.reshape(average.shape).astype(jnp.float32)
    return (weights.reshape(shards * groups * rows, cols), new_master, new_one, new_two, new_average)


def solution(mesh):
    state = P(("section", "shard", "tensor"), None)
    in_specs = (
        P("shard", "section", "tensor"),
        state,
        state,
        state,
        P(("section", "shard"), "tensor"),
        P(),
    )
    out_specs = (
        P("section", "tensor"),
        state,
        state,
        state,
        P(("section", "shard"), "tensor"),
    )
    fn = functools.partial(body, [(name, mesh.shape[name]) for name in ("tensor", "section", "shard")])
    return jax.shard_map(fn, mesh=mesh, in_specs=in_specs, out_specs=out_specs, check_vma=False)
```

```python
import functools
import math

import jax
import jax.numpy as jnp
from jax import lax
from jax.experimental import pallas as pl
from jax.experimental.pallas import tpu as pltpu
from jax.sharding import PartitionSpec as P

D = 4096
QKV = 6144


def update_kernel(pos, scal, grad, master, one, two, out_master, out_one, out_two, out_half):
    clip, first_fix, second_fix = scal[0], scal[1], scal[2]
    clipped = clip * grad[0].astype(jnp.float32)
    new_one = 0.9 * one[...] + 0.1 * clipped
    new_two = 0.95 * two[...] + 0.05 * clipped * clipped
    update = new_one / first_fix / (jnp.sqrt(new_two / second_fix) + 1e-08)
    new_master = master[...] * (1.0 - 0.1 * 0.1) - 0.1 * update
    out_one[...] = new_one
    out_two[...] = new_two
    out_master[...] = new_master
    out_half[0] = new_master.astype(jnp.bfloat16)


def update(pos, scal, grads, master, one, two):
    groups, rows, cols = grads.shape
    tile = min(rows, 32)
    state = pl.BlockSpec((tile, cols), lambda k, r, p: (r, lax.rem(p[0] - k + groups, groups)))
    piece = pl.BlockSpec((1, tile, cols), lambda k, r, p: (k, r, 0))
    return pl.pallas_call(
        update_kernel,
        grid_spec=pltpu.PrefetchScalarGridSpec(
            num_scalar_prefetch=1,
            grid=(groups, rows // tile),
            in_specs=[pl.BlockSpec(memory_space=pltpu.SMEM), piece, state, state, state],
            out_specs=[state, state, state, piece],
        ),
        out_shape=[jax.ShapeDtypeStruct(master.shape, jnp.float32)] * 3
        + [jax.ShapeDtypeStruct(grads.shape, jnp.bfloat16)],
        compiler_params=pltpu.CompilerParams(vmem_limit_bytes=32 * 2**20),
        cost_estimate=pl.CostEstimate(flops=master.size * 16, bytes_accessed=master.size * 28, transcendentals=0),
    )(pos, scal, grads, master, one, two)


MESH = pl.DeviceIdType.MESH


def total_kernel(axes, x_ref, out_ref, held, send_sem, recv_sem):
    barrier = pltpu.get_barrier_semaphore()
    count = 0
    for name, size in axes:
        me = lax.axis_index(name)
        for off in range(1, size):
            pl.semaphore_signal(
                barrier, inc=1, device_id={name: lax.rem(me + off, size)}, device_id_type=MESH
            )
            count += 1
    pl.semaphore_wait(barrier, count)
    at = 0
    own = x_ref[...]
    for name, size in axes:
        me = lax.axis_index(name)
        held[at] = own
        copies = []
        for off in range(1, size):
            copy = pltpu.make_async_remote_copy(
                src_ref=held.at[at],
                dst_ref=held.at[at + off],
                send_sem=send_sem.at[at + off],
                recv_sem=recv_sem.at[at + off],
                device_id={name: lax.rem(me + off, size)},
                device_id_type=MESH,
            )
            copy.start()
            copies.append(copy)
        for off, copy in enumerate(copies, 1):
            copy.wait()
            own = own + held[at + off]
        at += size
    out_ref[...] = own


def total(axes, value):
    slots = sum(size for _, size in axes)
    return pl.pallas_call(
        functools.partial(total_kernel, axes),
        out_shape=jax.ShapeDtypeStruct((8, 128), jnp.float32),
        in_specs=[pl.BlockSpec(memory_space=pltpu.VMEM)],
        out_specs=pl.BlockSpec(memory_space=pltpu.VMEM),
        scratch_shapes=[
            pltpu.VMEM((slots, 8, 128), jnp.float32),
            pltpu.SemaphoreType.DMA((slots,)),
            pltpu.SemaphoreType.DMA((slots,)),
        ],
        compiler_params=pltpu.CompilerParams(collective_id=0, has_side_effects=True),
    )(jnp.full((8, 128), value, jnp.float32))[0, 0]


def spread_kernel(shards, groups, half, out, y_send, y_recv, z_send, z_recv, own_sem):
    s = lax.axis_index("shard")
    t = lax.axis_index("tensor")
    last = shards - 1
    barrier = pltpu.get_barrier_semaphore()
    for off in range(1, groups):
        pl.semaphore_signal(
            barrier, inc=1, device_id={"tensor": lax.rem(t + off, groups)}, device_id_type=MESH
        )

    @pl.when(s < last)
    def _():
        pl.semaphore_signal(barrier, inc=1, device_id={"shard": s + 1}, device_id_type=MESH)

    @pl.when(s > 0)
    def _():
        pl.semaphore_signal(barrier, inc=1, device_id={"shard": s - 1}, device_id_type=MESH)

    peers = groups - 1 + jnp.minimum(s, 1) + jnp.minimum(last - s, 1)
    pl.semaphore_wait(barrier, peers)

    def across(k):
        return pltpu.make_async_remote_copy(
            src_ref=half.at[k],
            dst_ref=out.at[s, t],
            send_sem=y_send.at[k],
            recv_sem=y_recv.at[k],
            device_id={"tensor": lax.rem(t - k + groups, groups)},
            device_id_type=MESH,
        )

    def hop(way, k, d):
        slot = s - d if way == 0 else s + d
        group = lax.rem(t + k, groups)
        return pltpu.make_async_remote_copy(
            src_ref=half.at[0] if k == 0 and d == 0 else out.at[slot, group],
            dst_ref=out.at[slot, group],
            send_sem=z_send.at[way, k, d],
            recv_sem=z_recv.at[way, k, d],
            device_id={"shard": s + 1 if way == 0 else s - 1},
            device_id_type=MESH,
        )

    def arrival(way, k, d):
        slot = s - d if way == 0 else s + d
        group = lax.rem(t + k, groups)
        return pltpu.make_async_remote_copy(
            src_ref=out.at[slot, group],
            dst_ref=out.at[slot, group],
            send_sem=z_send.at[way, k, d - 1],
            recv_sem=z_recv.at[way, k, d - 1],
            device_id={"shard": s - 1 if way == 0 else s + 1},
            device_id_type=MESH,
        )

    def sends(way, d):
        if way == 0:
            return jnp.logical_and(s >= d, s < last)
        return jnp.logical_and(s + d <= last, s > 0)

    def gets(way, d):
        return s >= d if way == 0 else s + d <= last

    order = sorted(((k, d) for k in range(groups) for d in range(shards)), key=lambda e: (e[0] + e[1], e[0]))
    for k, d in order:
        if d == 0 and k:
            landed = pltpu.make_async_remote_copy(
                src_ref=half.at[k],
                dst_ref=out.at[s, lax.rem(t + k, groups)],
                send_sem=y_send.at[k],
                recv_sem=y_recv.at[k],
                device_id={"tensor": lax.rem(t + k, groups)},
                device_id_type=MESH,
            )
            landed.wait_recv()
        for way in (0, 1):
            if d:
                @pl.when(gets(way, d))
                def _():
                    arrival(way, k, d).wait_recv()
            if d < last:
                @pl.when(sends(way, d))
                def _():
                    hop(way, k, d).start()
        if d == 0 and k == 0:
            for j in range(1, groups):
                across(j).start()
            pltpu.make_async_copy(half.at[0], out.at[s, t], own_sem).start()
    pltpu.make_async_copy(half.at[0], out.at[s, t], own_sem).wait()
    for k, d in order:
        if d == 0 and k:
            across(k).wait_send()
        for way in (0, 1):
            if d < last:
                @pl.when(sends(way, d))
                def _():
                    hop(way, k, d).wait_send()


def spread(shards, groups, half):
    _, rows, cols = half.shape
    return pl.pallas_call(
        functools.partial(spread_kernel, shards, groups),
        out_shape=jax.ShapeDtypeStruct((shards, groups, rows, cols), half.dtype),
        in_specs=[pl.BlockSpec(memory_space=pl.ANY)],
        out_specs=pl.BlockSpec(memory_space=pl.ANY),
        scratch_shapes=[
            pltpu.SemaphoreType.DMA((groups,)),
            pltpu.SemaphoreType.DMA((groups,)),
            pltpu.SemaphoreType.DMA((2, groups, shards)),
            pltpu.SemaphoreType.DMA((2, groups, shards)),
            pltpu.SemaphoreType.DMA,
        ],
        compiler_params=pltpu.CompilerParams(collective_id=1, has_side_effects=True),
    )(half)


def reduce_kernel(shards, groups, x, out, square, inbox, own, ybox, z_send, z_recv, y_send, y_recv):
    s = lax.axis_index("shard")
    t = lax.axis_index("tensor")
    last = shards - 1
    rows = x.shape[2]
    tile = min(rows, 16)
    barrier = pltpu.get_barrier_semaphore()
    for off in range(1, groups):
        pl.semaphore_signal(
            barrier, inc=1, device_id={"tensor": lax.rem(t + off, groups)}, device_id_type=MESH
        )

    @pl.when(s < last)
    def _():
        pl.semaphore_signal(barrier, inc=1, device_id={"shard": s + 1}, device_id_type=MESH)

    @pl.when(s > 0)
    def _():
        pl.semaphore_signal(barrier, inc=1, device_id={"shard": s - 1}, device_id_type=MESH)

    peers = groups - 1 + jnp.minimum(s, 1) + jnp.minimum(last - s, 1)
    pl.semaphore_wait(barrier, peers)
    square[...] = jnp.zeros_like(square)

    def hop(way, k, q, first):
        return pltpu.make_async_remote_copy(
            src_ref=x.at[q, lax.rem(t + k, groups)] if first else inbox.at[way, k, q],
            dst_ref=inbox.at[way, k, q],
            send_sem=z_send.at[way, k, q],
            recv_sem=z_recv.at[way, k, q],
            device_id={"shard": s + 1 if way == 0 else s - 1},
            device_id_type=MESH,
        )

    def arrival(way, k, q):
        return pltpu.make_async_remote_copy(
            src_ref=inbox.at[way, k, q],
            dst_ref=inbox.at[way, k, q],
            send_sem=z_send.at[way, k, q],
            recv_sem=z_recv.at[way, k, q],
            device_id={"shard": s - 1 if way == 0 else s + 1},
            device_id_type=MESH,
        )

    def roles(way, q):
        if way == 0:
            return jnp.logical_and(s == 0, q > 0), jnp.logical_and(s > 0, s < q)
        return jnp.logical_and(s == last, q < last), jnp.logical_and(s < last, s > q)

    def forward(way, k, q):
        first, middle = roles(way, q)
        group = lax.rem(t + k, groups)

        @pl.when(first)
        def _():
            hop(way, k, q, True).start()

        @pl.when(middle)
        def _():
            arrival(way, k, q).wait_recv()

            @pl.loop(0, rows // tile)
            def _(i):
                part = pl.ds(pl.multiple_of(i * tile, tile), tile)
                both = inbox[way, k, q, part].astype(jnp.float32) + x[q, group, part].astype(jnp.float32)
                inbox[way, k, q, part] = both.astype(jnp.bfloat16)

            hop(way, k, q, False).start()

    def across(k):
        return pltpu.make_async_remote_copy(
            src_ref=own.at[k],
            dst_ref=ybox.at[k],
            send_sem=y_send.at[k],
            recv_sem=y_recv.at[k],
            device_id={"tensor": lax.rem(t + k, groups)},
            device_id_type=MESH,
        )

    def finish(k):
        group = lax.rem(t + k, groups)
        for q in range(shards):
            @pl.when(s == q)
            def _():
                ways = [way for way in (0, 1) if (q > 0 if way == 0 else q < last)]
                for way in ways:
                    arrival(way, k, q).wait_recv()

                @pl.loop(0, rows // tile)
                def _(i):
                    part = pl.ds(pl.multiple_of(i * tile, tile), tile)
                    acc = x[q, group, part].astype(jnp.float32)
                    for way in ways:
                        acc = acc + inbox[way, k, q, part].astype(jnp.float32)
                    own[k, part] = acc.astype(jnp.bfloat16)
                    square[...] += jnp.sum((acc * acc).reshape(tile // 8, 8, acc.shape[1]), axis=0)

        if k:
            across(k).start()

    pairs = [(way, j) for j in range(last) for way in (0, 1)]
    for k in range(groups - 1, -1, -1):
        for n, (way, j) in enumerate(pairs):
            forward(way, k, last - j if way == 0 else j)
            if n == 1 and k < groups - 1:
                finish(k + 1)
    finish(0)
    out[0] = own[0]
    for k in range(1, groups):
        across(k).wait_recv()
        out[k] = ybox[k]
        across(k).wait_send()
    for k in range(groups):
        for way in (0, 1):
            for q in range(shards):
                first, middle = roles(way, q)

                @pl.when(jnp.logical_or(first, middle))
                def _():
                    hop(way, k, q, False).wait_send()


def reduce_shares(shards, groups, x):
    _, _, rows, cols = x.shape
    whole = pl.BlockSpec(memory_space=pltpu.VMEM)
    return pl.pallas_call(
        functools.partial(reduce_kernel, shards, groups),
        out_shape=[
            jax.ShapeDtypeStruct((groups, rows, cols), jnp.bfloat16),
            jax.ShapeDtypeStruct((8, cols), jnp.float32),
        ],
        in_specs=[whole],
        out_specs=[whole, whole],
        scratch_shapes=[
            pltpu.VMEM((2, groups, shards, rows, cols), jnp.bfloat16),
            pltpu.VMEM((groups, rows, cols), jnp.bfloat16),
            pltpu.VMEM((groups, rows, cols), jnp.bfloat16),
            pltpu.SemaphoreType.DMA((2, groups, shards)),
            pltpu.SemaphoreType.DMA((2, groups, shards)),
            pltpu.SemaphoreType.DMA((groups,)),
            pltpu.SemaphoreType.DMA((groups,)),
        ],
        compiler_params=pltpu.CompilerParams(
            collective_id=2, has_side_effects=True, vmem_limit_bytes=48 * 2**20
        ),
    )(x)


def body(axes, qkv_grad, master, moment_one, moment_two, average, step):
    shards, groups = dict(axes)["shard"], dict(axes)["tensor"]
    t = lax.axis_index("tensor")
    pos = jnp.reshape(t, (1,)).astype(jnp.int32)
    rows = qkv_grad.shape[1] // (shards * groups)
    cols = qkv_grad.shape[2]
    blocks = qkv_grad.reshape(shards, groups, rows, cols)
    pieces, square = reduce_shares(shards, groups, blocks)
    local_sq = jnp.sum(square)
    sumsq = total(axes, local_sq)
    limit = jnp.float32(math.sqrt(D * QKV))
    clip = jnp.minimum(jnp.float32(1.0), limit / (jnp.sqrt(sumsq) + 1e-06))
    count = step.astype(jnp.float32)
    first_fix = 1.0 - jnp.power(jnp.float32(0.9), count)
    second_fix = 1.0 - jnp.power(jnp.float32(0.95), count)
    scal = jnp.stack([clip, first_fix, second_fix])
    new_master, new_one, new_two, half = update(
        pos, scal, pieces, master, moment_one, moment_two
    )
    weights = spread(shards, groups, half)
    fresh = lax.dynamic_index_in_dim(weights, lax.axis_index("shard"), 0, keepdims=False)
    new_average = 0.99 * average + 0.01 * fresh.reshape(average.shape).astype(jnp.float32)
    return (weights.reshape(shards * groups * rows, cols), new_master, new_one, new_two, new_average)


def solution(mesh):
    state = P(("section", "shard", "tensor"), None)
    in_specs = (
        P("shard", "section", "tensor"),
        state,
        state,
        state,
        P(("section", "shard"), "tensor"),
        P(),
    )
    out_specs = (
        P("section", "tensor"),
        state,
        state,
        state,
        P(("section", "shard"), "tensor"),
    )
    fn = functools.partial(body, [(name, mesh.shape[name]) for name in ("tensor", "section", "shard")])
    return jax.shard_map(fn, mesh=mesh, in_specs=in_specs, out_specs=out_specs, check_vma=False)
```
